32 devices in a mesh: groups: 2 (over x), tile: 8 (over z, y), rot: 2 (over core).
Axes of the slice: x: 2, y: 2, z: 4, core: 2. Of those that a mesh axis runs over, the one named last changes fastest.
Arguments:
- features: bfloat16 [256, 512, 8, 64], P(('groups', 'tile'), None, 'rot'), parts along dimension 0, may hold values from -6 to 6
- weight: bfloat16 [8, 9, 64, 64], replicated, may hold values from -0.09375 to 0.09375
- bias: float32 [64], replicated, may hold values from -1 to 1
Outputs:
- output: bfloat16 [256, 512, 8, 64], P(('groups', 'tile'), None, 'rot'), parts along dimension 0
The draws below stay inside these ranges and needn't reach their ends.
There are 2 independent parts, one for each index of `groups`. The reference program is written for one: setup_inputs(seed, part) draws one part's arguments, and reference() takes and returns one part's arrays. A program takes and returns all parts, laid end to end along the dimension named above; an argument that names none is the same for every part. Nothing has to cross between parts.
All inputs are finite; a program needn't handle non-finite values.
Results may differ from the reference program's by a relative error of at most 0.001.
Values may be sent and summed in bfloat16 or wider, within the bound.
No kernel may reach another device: no remote copies, remote signals or barrier semaphores. Data moves between devices by JAX's collectives and lax.ppermute only.
A program may use at most 256 MiB of HBM per device.

```python
import jax
import jax.numpy as jnp
import numpy as np
from jax import lax

C = 64
ORIENT = 8
COLS = 512
HEIGHT = 128


def shard_levels(stream_key, shape, shards, least, top_value):
    factor_of, own = 1.0, jax.random.fold_in(stream_key, 6)
    for dim, blocks in shards:
        steps = jnp.exp(jax.random.uniform(jax.random.fold_in(own, dim), (blocks,), jnp.float32, least / len(shards), top_value / len(shards)))
        factor_of = factor_of * jnp.repeat(steps, shape[dim] // blocks).reshape([-1 if axis == dim else 1 for axis in range(len(shape))])
    return factor_of


def bell_draw(key, shape, deviation, reach, pieces=(), kind=jnp.bfloat16):
    entries = deviation * jax.random.normal(key, shape, jnp.float32)
    if pieces:
        entries = entries * shard_levels(key, shape, pieces, -0.22, 0.18)
    return jnp.clip(entries, -reach, reach).astype(kind)


def setup_inputs(seed: int = 0, part: int = 0) -> dict:
    key_list = jax.random.split(jax.random.key(seed), 4)
    part_splits = jax.random.split(jax.random.fold_in(key_list[3], part), 4)
    features = bell_draw(part_splits[0], (HEIGHT, COLS, ORIENT, C), 1.0, 6.0, ((0, 8), (2, 2)))
    weight = bell_draw(key_list[1], (ORIENT, 9, C, C), (9 * ORIENT * C) ** -0.5, 0.09375)
    bias = jnp.clip(jax.random.uniform(key_list[2], (C,), jnp.float32, -1.0, 1.0), -1.0, 1.0)
    return dict(features=features, weight=weight, bias=bias)


def source_table():
    cycle = [5, 2, 1, 0, 3, 6, 7, 8]
    table = np.zeros((8, 9), np.int32)
    for turn in range(8):
        table[turn, 4] = 4
        for place in range(8):
            table[turn, cycle[place]] = cycle[(place - turn) % 8]
    return table


def reference(features, weight, bias):
    height, cols, orient, chans = features.shape
    padded = jnp.pad(features.astype(jnp.float32), ((1, 1), (1, 1), (0, 0), (0, 0)))
    table = source_table()
    weight_full = weight.astype(jnp.float32)
    results = []
    for turn in range(8):
        relative = (np.arange(8) - turn) % 8
        filters = weight_full[relative][:, table[turn]]
        total = jnp.zeros((height * cols, chans), jnp.float32)
        for row_off in range(3):
            for col_off in range(3):
                tap = row_off * 3 + col_off
                window = padded[row_off:row_off + height, col_off:col_off + cols].reshape(height * cols, orient * chans)
                total = total + jnp.dot(window, filters[:, tap].reshape(orient * chans, chans), preferred_element_type=jnp.float32, precision=lax.Precision.HIGHEST)
        results.append(jnp.maximum(total + bias[None, :], 0.0).reshape(height, cols, chans))
    return jnp.stack(results, 2).astype(jnp.bfloat16)
```

```python
import functools

import jax
import jax.numpy as jnp
import numpy as np
from jax import lax
from jax.experimental import pallas as pl
from jax.experimental.pallas import tpu as pltpu
from jax.sharding import PartitionSpec as P


def source_table():
    cycle = [5, 2, 1, 0, 3, 6, 7, 8]
    table = np.zeros((8, 9), np.int32)
    for turn in range(8):
        table[turn, 4] = 4
        for place in range(8):
            table[turn, cycle[place]] = cycle[(place - turn) % 8]
    return table


def filter_kernel(owned, orient, here_ref, weight_ref, out_ref):
    chans = weight_ref.shape[3]
    table = source_table()
    flip = here_ref[0] == 1
    for rel in range(orient):
        for tap in range(9):
            nxt = (rel + 1) % orient
            pair = jnp.concatenate([weight_ref[rel, tap], weight_ref[nxt, tap]], 0)
            turned = jnp.transpose(pair)
            for r in range(owned):
                near = int(np.argwhere(table[r] == tap)[0, 0])
                far = int(np.argwhere(table[r + owned] == tap)[0, 0])
                where = near if near == far else jnp.where(flip, far, near)
                for half in range(2):
                    for s in range(0, owned, 2):
                        if (s - r + half * owned) % orient == rel:
                            lane = (half * owned + s) * chans
                            out_ref[where, r * chans : (r + 1) * chans, lane : lane + 2 * chans] = turned


def build_filters(weight, here, owned):
    orient, taps, chans, width = weight.shape
    vmem = pl.BlockSpec(memory_space=pltpu.VMEM)
    return pl.pallas_call(
        functools.partial(filter_kernel, owned, orient),
        out_shape=jax.ShapeDtypeStruct((taps, owned * width, orient * chans), weight.dtype),
        in_specs=[pl.BlockSpec(memory_space=pltpu.SMEM), vmem],
        out_specs=vmem,
        name="filters",
    )(here, weight)


def shifted(x, step):
    cols = x.shape[1]
    place = lax.broadcasted_iota(jnp.int32, x.shape, 1) + step
    turned = pltpu.roll(x, (-step) % cols, 1)
    return jnp.where((place >= 0) & (place < cols), turned, jnp.zeros_like(turned))


def conv_kernel(
    filt_hbm, bias_ref, own_hbm, other_hbm, halo_hbm, halo_other_hbm, out_hbm,
    filt, x, out, filt_sem, in_sem, out_sem,
):
    rows = own_hbm.shape[0]
    half = own_hbm.shape[1]
    load_filt = pltpu.make_async_copy(filt_hbm, filt, filt_sem)
    load_filt.start()

    def load(j, which, src):
        lane = slice(which * half, (which + 1) * half)
        return pltpu.make_async_copy(src, x.at[j, lane], in_sem.at[which, j])

    load(0, 0, halo_hbm.at[0]).start()
    load(0, 1, halo_other_hbm.at[0]).start()

    def issue(j, carry):
        load(j + 1, 0, own_hbm.at[j]).start()
        load(j + 1, 1, other_hbm.at[j]).start()
        return carry

    lax.fori_loop(0, rows, issue, 0)
    load(rows + 1, 0, halo_hbm.at[1]).start()
    load(rows + 1, 1, halo_other_hbm.at[1]).start()

    def arrived(j):
        load(j, 0, own_hbm.at[0]).wait()
        load(j, 1, other_hbm.at[0]).wait()

    arrived(0)
    arrived(1)
    load_filt.wait()
    bias_col = bias_ref[...]

    def body(i, carry):
        for k in range(2):
            arrived(2 * i + k + 2)
        for k in range(2):
            y = 2 * i + k
            acc = None
            for a in range(3):
                line = x[y + a]
                for b in range(3):
                    term = jnp.dot(
                        filt[3 * a + b],
                        line if b == 1 else shifted(line, b - 1),
                        preferred_element_type=jnp.float32,
                    )
                    acc = term if acc is None else acc + term
            out[y] = jnp.maximum(acc + bias_col, 0.0).astype(out.dtype)
            pltpu.make_async_copy(out.at[y], out_hbm.at[y], out_sem).start()
        return carry

    lax.fori_loop(0, rows // 2, body, 0)
    pltpu.make_async_copy(out, out_hbm, out_sem).wait()


def convolve(filt, bias_col, own, other, halo, halo_other):
    rows, half, cols = own.shape
    hbm = pl.BlockSpec(memory_space=pl.ANY)
    vmem = pl.BlockSpec(memory_space=pltpu.VMEM)
    return pl.pallas_call(
        conv_kernel,
        out_shape=jax.ShapeDtypeStruct((rows, filt.shape[1], cols), jnp.bfloat16),
        in_specs=[hbm, vmem, hbm, hbm, hbm, hbm],
        out_specs=hbm,
        scratch_shapes=[
            pltpu.VMEM(filt.shape, filt.dtype),
            pltpu.VMEM((rows + 2, 2 * half, cols), own.dtype),
            pltpu.VMEM((rows, filt.shape[1], cols), jnp.bfloat16),
            pltpu.SemaphoreType.DMA,
            pltpu.SemaphoreType.DMA((2, rows + 2)),
            pltpu.SemaphoreType.DMA,
        ],
        compiler_params=pltpu.CompilerParams(vmem_limit_bytes=56 << 20),
        name="convolve",
    )(filt, bias_col, own, other, halo, halo_other)


def local(features, weight, bias):
    rows, cols, owned, chans = features.shape
    count = lax.axis_size("tile")
    swap = [(0, 1), (1, 0)]
    here = lax.axis_index("rot").astype(jnp.int32).reshape(1)
    own = jnp.transpose(features, (0, 2, 3, 1)).reshape(rows, owned * chans, cols)
    above = lax.ppermute(own[rows - 1 :], "tile", [(i, i + 1) for i in range(count - 1)])
    below = lax.ppermute(own[:1], "tile", [(i + 1, i) for i in range(count - 1)])
    other = lax.ppermute(own, "rot", swap)
    halo = jnp.concatenate([above, below], 0)
    halo_other = lax.ppermute(halo, "rot", swap)
    filt = build_filters(weight, here, owned)
    bias_col = jnp.tile(bias, owned).reshape(owned * chans, 1)
    out = convolve(filt, bias_col, own, other, halo, halo_other)
    return jnp.transpose(out.reshape(rows, owned, chans, cols), (0, 3, 1, 2))


def solution(mesh):
    spec = P(("groups", "tile"), None, "rot", None)
    return jax.shard_map(
        local,
        mesh=mesh,
        in_specs=(spec, P(), P()),
        out_specs=spec,
        check_vma=False,
    )
```

```python
import functools

import jax
import jax.numpy as jnp
import numpy as np
from jax import lax
from jax.experimental import pallas as pl
from jax.experimental.pallas import tpu as pltpu
from jax.sharding import PartitionSpec as P

VMEM = pl.BlockSpec(memory_space=pltpu.VMEM)
HBM = pl.BlockSpec(memory_space=pltpu.HBM)


def source_table():
    cycle = [5, 2, 1, 0, 3, 6, 7, 8]
    table = np.zeros((8, 9), np.int32)
    for turn in range(8):
        table[turn, 4] = 4
        for place in range(8):
            table[turn, cycle[place]] = cycle[(place - turn) % 8]
    return table


def filters_kernel(owned, orient, weight_ref, bias_ref, filt_ref, column_ref):
    chans = weight_ref.shape[3]
    table = source_table()
    flip = lax.axis_index("rot") == 1
    for rel in range(orient):
        for tap in range(9):
            pair = jnp.concatenate([weight_ref[rel, tap], weight_ref[(rel + 1) % orient, tap]], 0)
            turned = jnp.transpose(pair)
            for r in range(owned):
                here = int(np.argwhere(table[r] == tap)[0, 0])
                there = int(np.argwhere(table[r + owned] == tap)[0, 0])
                where = here if here == there else jnp.where(flip, there, here)
                for half in range(2):
                    for s in range(0, owned, 2):
                        if (s - r + half * owned) % orient == rel:
                            lane = (half * owned + s) * chans
                            filt_ref[where, r * chans : (r + 1) * chans, lane : lane + 2 * chans] = turned
    wide = jnp.broadcast_to(bias_ref[...], (128, chans))
    column_ref[...] = jnp.concatenate([jnp.transpose(wide)] * owned, 0)


def build_filters(weight, bias, owned):
    orient, taps, chans, width = weight.shape
    return pl.pallas_call(
        functools.partial(filters_kernel, owned, orient),
        out_shape=(
            jax.ShapeDtypeStruct((taps, owned * width, orient * chans), weight.dtype),
            jax.ShapeDtypeStruct((owned * width, 128), jnp.float32),
        ),
        in_specs=[VMEM, VMEM],
        out_specs=(VMEM, VMEM),
        compiler_params=pltpu.CompilerParams(vmem_limit_bytes=12 << 20),
        name="filters",
    )(weight, bias)


def pick_kernel(own, near, far, near_sem, far_sem):
    rows = own.shape[0]
    even = lax.rem(lax.axis_index("tile"), 2) == 0
    first = jnp.where(even, rows - 1, 0)
    send_near = pltpu.make_async_copy(own.at[pl.ds(first, 1)], near, near_sem)
    send_far = pltpu.make_async_copy(own.at[pl.ds(rows - 1 - first, 1)], far, far_sem)
    send_near.start()
    send_far.start()
    send_near.wait()
    send_far.wait()


def pick_edges(own):
    edge = jax.ShapeDtypeStruct((1,) + own.shape[1:], own.dtype)
    return pl.pallas_call(
        pick_kernel,
        out_shape=(edge, edge),
        in_specs=[HBM],
        out_specs=(VMEM, VMEM),
        scratch_shapes=[pltpu.SemaphoreType.DMA, pltpu.SemaphoreType.DMA],
        compiler_params=pltpu.CompilerParams(vmem_limit_bytes=4 << 20),
        name="pick",
    )(pltpu.with_memory_space_constraint(own, pltpu.HBM))


def shifted(x, step):
    cols = x.shape[1]
    place = lax.broadcasted_iota(jnp.int32, x.shape, 1) + step
    turned = pltpu.roll(x, (-step) % cols, 1)
    return jnp.where((place >= 0) & (place < cols), turned, jnp.zeros_like(turned))


def row_sums(filt, lines, column):
    half = filt.shape[2] // 2
    acc = None
    for b in (1, 0, 2):
        for a, line in enumerate(lines):
            for which, part in enumerate(line):
                term = jnp.dot(
                    filt[3 * a + b, :, which * half : (which + 1) * half],
                    part if b == 1 else shifted(part, b - 1),
                    preferred_element_type=jnp.float32,
                )
                acc = term if acc is None else acc + term
    wide = jnp.concatenate([column] * (acc.shape[1] // column.shape[1]), 1)
    return jnp.maximum(acc + wide, 0.0).astype(jnp.bfloat16)


def inner_kernel(first, last, filt, column, own, other, *rest):
    out_hbm, out, out_sem = rest[-3:]
    for y in range(first, last):
        lines = [(own[y + a - 1], other[y + a - 1]) for a in range(3)]
        out[y - first] = row_sums(filt, lines, column[...])
        pltpu.make_async_copy(out.at[y - first], out_hbm.at[y], out_sem).start()
    pltpu.make_async_copy(out, out_hbm.at[pl.ds(first, last - first)], out_sem).wait()


def inner(first, last, filt, column, own, other, partial=None):
    rows, half, cols = own.shape
    count = last - first
    flops = 2 * count * cols * filt.shape[0] * filt.shape[1] * filt.shape[2]
    extra = [] if partial is None else [partial]
    return pl.pallas_call(
        functools.partial(inner_kernel, first, last),
        out_shape=jax.ShapeDtypeStruct((rows, filt.shape[1], cols), jnp.bfloat16),
        in_specs=[VMEM] * 4 + [HBM] * len(extra),
        out_specs=HBM,
        scratch_shapes=[
            pltpu.VMEM((count, filt.shape[1], cols), jnp.bfloat16),
            pltpu.SemaphoreType.DMA,
        ],
        input_output_aliases={4: 0} if extra else {},
        compiler_params=pltpu.CompilerParams(vmem_limit_bytes=20 << 20),
        cost_estimate=pl.CostEstimate(flops=flops, bytes_accessed=count * half * cols * 6, transcendentals=0),
        name="inner",
    )(filt, column, own, other, *extra)


def edge_kernel(filt, column, own, other, near_own, near_other, far_own, far_other, partial, out_hbm, out, out_sem):
    rows = own.shape[0]
    even = lax.rem(lax.axis_index("tile"), 2) == 0
    pairs = ((near_own[0], far_own[0]), (near_other[0], far_other[0]))
    above = [jnp.where(even, far, near) for near, far in pairs]
    below = [jnp.where(even, near, far) for near, far in pairs]
    sends = []
    for k, y in enumerate((0, rows - 1)):
        body = [(own[j], other[j]) for j in ((0, 1), (rows - 2, rows - 1))[k]]
        out[k] = row_sums(filt, [above] + body if k == 0 else body + [below], column[...])
        sends.append(pltpu.make_async_copy(out.at[k], out_hbm.at[y], out_sem.at[k]))
        sends[-1].start()
    for send in sends:
        send.wait()


def edges(filt, column, own, other, near_own, near_other, far_own, far_other, partial):
    rows, half, cols = own.shape
    return pl.pallas_call(
        edge_kernel,
        out_shape=jax.ShapeDtypeStruct(partial.shape, partial.dtype),
        in_specs=[VMEM] * 8 + [HBM],
        out_specs=HBM,
        scratch_shapes=[
            pltpu.VMEM((2, filt.shape[1], cols), jnp.bfloat16),
            pltpu.SemaphoreType.DMA((2,)),
        ],
        input_output_aliases={8: 0},
        compiler_params=pltpu.CompilerParams(vmem_limit_bytes=20 << 20),
        name="edges",
    )(filt, column, own, other, near_own, near_other, far_own, far_other, partial)


def local(features, weight, bias):
    rows, cols, owned, chans = features.shape
    count = lax.axis_size("tile")
    swap = [(0, 1), (1, 0)]
    own = jnp.transpose(features, (0, 2, 3, 1)).reshape(rows, owned * chans, cols)
    other = lax.ppermute(own, "rot", swap)
    near, far = pick_edges(own)

    def pairs(start):
        return [p for k in range(start, count - 1, 2) for p in ((k, k + 1), (k + 1, k))]

    near_own = lax.ppermute(near, "tile", pairs(0))
    far_own = lax.ppermute(far, "tile", pairs(1))
    filt, column = build_filters(weight, bias.reshape(1, chans), owned)
    split = rows // 2
    out = inner(1, split, filt, column, own, other)
    near_own, far_own, out = lax.optimization_barrier((near_own, far_own, out))
    near_other = lax.ppermute(near_own, "rot", swap)
    far_other = lax.ppermute(far_own, "rot", swap)
    out = inner(split, rows - 1, filt, column, own, other, out)
    out = edges(filt, column, own, other, near_own, near_other, far_own, far_other, out)
    return jnp.transpose(out.reshape(rows, owned, chans, cols), (0, 3, 1, 2))


def solution(mesh):
    spec = P(("groups", "tile"), None, "rot", None)
    return jax.shard_map(
        local,
        mesh=mesh,
        in_specs=(spec, P(), P()),
        out_specs=spec,
        check_vma=False,
    )
```

```python
import functools

import jax
import jax.numpy as jnp
import numpy as np
from jax import lax
from jax.experimental import pallas as pl
from jax.experimental.pallas import tpu as pltpu
from jax.sharding import PartitionSpec as P

VMEM = pl.BlockSpec(memory_space=pltpu.VMEM)
HBM = pl.BlockSpec(memory_space=pltpu.HBM)


def source_table():
    cycle = [5, 2, 1, 0, 3, 6, 7, 8]
    table = np.zeros((8, 9), np.int32)
    for turn in range(8):
        table[turn, 4] = 4
        for place in range(8):
            table[turn, cycle[place]] = cycle[(place - turn) % 8]
    return table


def filters_kernel(owned, orient, weight_ref, bias_ref, filt_ref, column_ref):
    chans = weight_ref.shape[3]
    table = source_table()
    flip = lax.axis_index("rot") == 1
    for rel in range(orient):
        for tap in range(9):
            pair = jnp.concatenate([weight_ref[rel, tap], weight_ref[(rel + 1) % orient, tap]], 0)
            turned = jnp.transpose(pair)
            for r in range(owned):
                here = int(np.argwhere(table[r] == tap)[0, 0])
                there = int(np.argwhere(table[r + owned] == tap)[0, 0])
                where = here if here == there else jnp.where(flip, there, here)
                for half in range(2):
                    for s in range(0, owned, 2):
                        if (s - r + half * owned) % orient == rel:
                            lane = (half * owned + s) * chans
                            filt_ref[where, r * chans : (r + 1) * chans, lane : lane + 2 * chans] = turned
    wide = jnp.broadcast_to(bias_ref[...], (128, chans))
    column_ref[...] = jnp.concatenate([jnp.transpose(wide)] * owned, 0)


def build_filters(weight, bias, owned):
    orient, taps, chans, width = weight.shape
    return pl.pallas_call(
        functools.partial(filters_kernel, owned, orient),
        out_shape=(
            jax.ShapeDtypeStruct((taps, owned * width, orient * chans), weight.dtype),
            jax.ShapeDtypeStruct((owned * width, 128), jnp.float32),
        ),
        in_specs=[VMEM, VMEM],
        out_specs=(VMEM, VMEM),
        compiler_params=pltpu.CompilerParams(vmem_limit_bytes=12 << 20),
        name="filters",
    )(weight, bias)


def pick_kernel(own, weight_hbm, near, far, weight, sems):
    rows = own.shape[0]
    even = lax.rem(lax.axis_index("tile"), 2) == 0
    first = jnp.where(even, rows - 1, 0)
    copies = [
        pltpu.make_async_copy(own.at[pl.ds(first, 1)], near, sems.at[0]),
        pltpu.make_async_copy(own.at[pl.ds(rows - 1 - first, 1)], far, sems.at[1]),
        pltpu.make_async_copy(weight_hbm, weight, sems.at[2]),
    ]
    for copy in copies:
        copy.start()
    for copy in copies:
        copy.wait()


def pick_edges(own, weight):
    edge = jax.ShapeDtypeStruct((1,) + own.shape[1:], own.dtype)
    return pl.pallas_call(
        pick_kernel,
        out_shape=(edge, edge, jax.ShapeDtypeStruct(weight.shape, weight.dtype)),
        in_specs=[HBM, HBM],
        out_specs=(VMEM, VMEM, VMEM),
        scratch_shapes=[pltpu.SemaphoreType.DMA((3,))],
        compiler_params=pltpu.CompilerParams(vmem_limit_bytes=8 << 20),
        name="pick",
    )(*(pltpu.with_memory_space_constraint(array, pltpu.HBM) for array in (own, weight)))


def shifted(x, step):
    cols = x.shape[1]
    place = lax.broadcasted_iota(jnp.int32, x.shape, 1) + step
    turned = pltpu.roll(x, (-step) % cols, 1)
    return jnp.where((place >= 0) & (place < cols), turned, jnp.zeros_like(turned))


def row_sums(filt, lines, column):
    half = filt.shape[2] // 2
    acc = None
    for b in (1, 0, 2):
        for a, line in enumerate(lines):
            for which, part in enumerate(line):
                term = jnp.dot(
                    filt[3 * a + b, :, which * half : (which + 1) * half],
                    part if b == 1 else shifted(part, b - 1),
                    preferred_element_type=jnp.float32,
                )
                acc = term if acc is None else acc + term
    wide = jnp.concatenate([column] * (acc.shape[1] // column.shape[1]), 1)
    return jnp.maximum(acc + wide, 0.0).astype(jnp.bfloat16)


def send(held, out_hbm, start, sem):
    return pltpu.make_async_copy(held, out_hbm.at[pl.ds(start, held.shape[0])], sem)


def first_kernel(filt, column, own, other, held):
    for k in range(held.shape[0]):
        lines = [(own[k + a], other[k + a]) for a in range(3)]
        held[k] = row_sums(filt, lines, column[...])


def second_kernel(filt, column, own, other, done, out_hbm, held, sem):
    copy = send(done, out_hbm, 1, sem)
    copy.start()
    start = 1 + done.shape[0]
    for k in range(held.shape[0]):
        lines = [(own[start + k + a - 1], other[start + k + a - 1]) for a in range(3)]
        held[k] = row_sums(filt, lines, column[...])
    copy.wait()


def last_kernel(
    filt, column, own, other, near_own, near_other, far_own, far_other, done, partial, out_hbm, out, sem, out_sem
):
    rows = own.shape[0]
    copies = [send(done, out_hbm, rows - 1 - done.shape[0], sem)]
    copies[0].start()
    even = lax.rem(lax.axis_index("tile"), 2) == 0
    pairs = ((near_own[0], far_own[0]), (near_other[0], far_other[0]))
    above = [jnp.where(even, far, near) for near, far in pairs]
    below = [jnp.where(even, near, far) for near, far in pairs]
    for k, y in enumerate((0, rows - 1)):
        body = [(own[j], other[j]) for j in ((0, 1), (rows - 2, rows - 1))[k]]
        out[k] = row_sums(filt, [above] + body if k == 0 else body + [below], column[...])
        copies.append(pltpu.make_async_copy(out.at[k], out_hbm.at[y], out_sem.at[k]))
        copies[-1].start()
    for copy in copies:
        copy.wait()


def call(kernel, name, shapes, inputs, scratch, aliases, count):
    filt, column, own, other = inputs[:4]
    rows, half, cols = own.shape
    flops = 2 * count * cols * filt.shape[0] * filt.shape[1] * filt.shape[2]
    return pl.pallas_call(
        kernel,
        out_shape=shapes,
        in_specs=[VMEM] * (len(inputs) - len(aliases)) + [HBM] * len(aliases),
        out_specs=tuple(VMEM if shape.shape[0] < rows else HBM for shape in shapes),
        scratch_shapes=scratch,
        input_output_aliases=aliases,
        compiler_params=pltpu.CompilerParams(vmem_limit_bytes=16 << 20),
        cost_estimate=pl.CostEstimate(flops=flops, bytes_accessed=count * half * cols * 6, transcendentals=0),
        name=name,
    )(*inputs)


def local(features, weight, bias):
    rows, cols, owned, chans = features.shape
    count = lax.axis_size("tile")
    swap = [(0, 1), (1, 0)]
    own = jnp.transpose(features, (0, 2, 3, 1)).reshape(rows, owned * chans, cols)
    other = lax.ppermute(own, "rot", swap)
    near, far, weight = pick_edges(own, weight)

    def pairs(start):
        return [p for k in range(start, count - 1, 2) for p in ((k, k + 1), (k + 1, k))]

    near_own = lax.ppermute(near, "tile", pairs(0))
    far_own = lax.ppermute(far, "tile", pairs(1))
    filt, column = build_filters(weight, bias.reshape(1, chans), owned)
    split = rows // 2 + 1
    line = (owned * weight.shape[3], cols)

    def block(n):
        return jax.ShapeDtypeStruct((n,) + line, jnp.bfloat16)

    inputs = (filt, column, own, other)
    dma = pltpu.SemaphoreType.DMA
    (done,) = call(first_kernel, "first", (block(split - 1),), inputs, [], {}, split - 1)
    near_own, far_own, done = lax.optimization_barrier((near_own, far_own, done))
    near_other = lax.ppermute(near_own, "rot", swap)
    far_other = lax.ppermute(far_own, "rot", swap)
    more = rows - 1 - split
    out, done = call(second_kernel, "second", (block(rows), block(more)), inputs + (done,), [dma], {}, more)
    (out,) = call(
        last_kernel,
        "last",
        (block(rows),),
        inputs + (near_own, near_other, far_own, far_other, done, out),
        [pltpu.VMEM((2,) + line, jnp.bfloat16), dma, dma((2,))],
        {9: 0},
        2,
    )
    return jnp.transpose(out.reshape(rows, owned, chans, cols), (0, 3, 1, 2))


def solution(mesh):
    spec = P(("groups", "tile"), None, "rot", None)
    return jax.shard_map(
        local,
        mesh=mesh,
        in_specs=(spec, P(), P()),
        out_specs=spec,
        check_vma=False,
    )
```

```python
import functools

import jax
import jax.numpy as jnp
import numpy as np
from jax import lax
from jax.experimental import pallas as pl
from jax.experimental.pallas import tpu as pltpu
from jax.sharding import PartitionSpec as P

VMEM = pl.BlockSpec(memory_space=pltpu.VMEM)
HBM = pl.BlockSpec(memory_space=pltpu.HBM)


def source_table():
    cycle = [5, 2, 1, 0, 3, 6, 7, 8]
    table = np.zeros((8, 9), np.int32)
    for turn in range(8):
        table[turn, 4] = 4
        for place in range(8):
            table[turn, cycle[place]] = cycle[(place - turn) % 8]
    return table


def filters_kernel(owned, orient, weight_ref, bias_ref, filt_ref, column_ref):
    chans = weight_ref.shape[3]
    table = source_table()
    flip = lax.axis_index("rot") == 1
    for rel in range(orient):
        for tap in range(9):
            pair = jnp.concatenate([weight_ref[rel, tap], weight_ref[(rel + 1) % orient, tap]], 0)
            turned = jnp.transpose(pair)
            for r in range(owned):
                here = int(np.argwhere(table[r] == tap)[0, 0])
                there = int(np.argwhere(table[r + owned] == tap)[0, 0])
                where = here if here == there else jnp.where(flip, there, here)
                for half in range(2):
                    for s in range(0, owned, 2):
                        if (s - r + half * owned) % orient == rel:
                            lane = (half * owned + s) * chans
                            filt_ref[where, r * chans : (r + 1) * chans, lane : lane + 2 * chans] = turned
    wide = jnp.broadcast_to(bias_ref[...], (128, chans))
    column_ref[...] = jnp.concatenate([jnp.transpose(wide)] * owned, 0)


def build_filters(weight, bias, owned):
    orient, taps, chans, width = weight.shape
    return pl.pallas_call(
        functools.partial(filters_kernel, owned, orient),
        out_shape=(
            jax.ShapeDtypeStruct((taps, owned * width, orient * chans), weight.dtype),
            jax.ShapeDtypeStruct((owned * width, 128), jnp.float32),
        ),
        in_specs=[VMEM, VMEM],
        out_specs=(VMEM, VMEM),
        compiler_params=pltpu.CompilerParams(vmem_limit_bytes=12 << 20),
        name="filters",
    )(weight, bias)


def pick_kernel(own, weight_hbm, near, far, weight, sems):
    rows = own.shape[0]
    even = lax.rem(lax.axis_index("tile"), 2) == 0
    first = jnp.where(even, rows - 1, 0)
    copies = [
        pltpu.make_async_copy(own.at[pl.ds(first, 1)], near, sems.at[0]),
        pltpu.make_async_copy(own.at[pl.ds(rows - 1 - first, 1)], far, sems.at[1]),
        pltpu.make_async_copy(weight_hbm, weight, sems.at[2]),
    ]
    for copy in copies:
        copy.start()
    for copy in copies:
        copy.wait()


def pick_edges(own, weight):
    edge = jax.ShapeDtypeStruct((1,) + own.shape[1:], own.dtype)
    return pl.pallas_call(
        pick_kernel,
        out_shape=(edge, edge, jax.ShapeDtypeStruct(weight.shape, weight.dtype)),
        in_specs=[HBM, HBM],
        out_specs=(VMEM, VMEM, VMEM),
        scratch_shapes=[pltpu.SemaphoreType.DMA((3,))],
        compiler_params=pltpu.CompilerParams(vmem_limit_bytes=8 << 20),
        name="pick",
    )(*(pltpu.with_memory_space_constraint(array, pltpu.HBM) for array in (own, weight)))


def shifted(x, step):
    cols = x.shape[1]
    place = lax.broadcasted_iota(jnp.int32, x.shape, 1) + step
    turned = pltpu.roll(x, (-step) % cols, 1)
    return jnp.where((place >= 0) & (place < cols), turned, jnp.zeros_like(turned))


def row_sums(filt, lines, column, order=(0, 1, 2)):
    half = filt.shape[2] // 2
    acc = None
    for b in (1, 0, 2):
        for a in order:
            for which, part in enumerate(lines[a]):
                term = jnp.dot(
                    filt[3 * a + b, :, which * half : (which + 1) * half],
                    part if b == 1 else shifted(part, b - 1),
                    preferred_element_type=jnp.float32,
                )
                acc = term if acc is None else acc + term
    wide = jnp.concatenate([column] * (acc.shape[1] // column.shape[1]), 1)
    return jnp.maximum(acc + wide, 0.0).astype(jnp.bfloat16)


def send(held, out_hbm, start, sem):
    return pltpu.make_async_copy(held, out_hbm.at[pl.ds(start, held.shape[0])], sem)


def first_kernel(filt, column, own, other, held):
    for k in range(held.shape[0]):
        lines = [(own[k + a], other[k + a]) for a in range(3)]
        held[k] = row_sums(filt, lines, column[...])


def second_kernel(filt, column, own, other, done, out_hbm, held, sem):
    copy = send(done, out_hbm, 1, sem)
    copy.start()
    start = 1 + done.shape[0]
    for k in range(held.shape[0]):
        lines = [(own[start + k + a - 1], other[start + k + a - 1]) for a in range(3)]
        held[k] = row_sums(filt, lines, column[...])
    copy.wait()


def last_kernel(
    filt, column, own, other, halo, halo_other, done, partial, out_hbm, out, sem, out_sem
):
    rows = own.shape[0]
    copies = [send(done, out_hbm, rows - 1 - done.shape[0], sem)]
    copies[0].start()
    even = lax.rem(lax.axis_index("tile"), 2) == 0
    pairs = ((halo[0], halo[1]), (halo_other[0], halo_other[1]))
    above = [jnp.where(even, far, near) for near, far in pairs]
    below = [jnp.where(even, near, far) for near, far in pairs]
    for k, y in enumerate((0, rows - 1)):
        body = [(own[j], other[j]) for j in ((0, 1), (rows - 2, rows - 1))[k]]
        lines = [above] + body if k == 0 else body + [below]
        out[k] = row_sums(filt, lines, column[...], (1, 2, 0) if k == 0 else (0, 1, 2))
        copies.append(pltpu.make_async_copy(out.at[k], out_hbm.at[y], out_sem.at[k]))
        copies[-1].start()
    for copy in copies:
        copy.wait()


def call(kernel, name, shapes, inputs, scratch, aliases, count):
    filt, column, own, other = inputs[:4]
    rows, half, cols = own.shape
    flops = 2 * count * cols * filt.shape[0] * filt.shape[1] * filt.shape[2]
    return pl.pallas_call(
        kernel,
        out_shape=shapes,
        in_specs=[VMEM] * (len(inputs) - len(aliases)) + [HBM] * len(aliases),
        out_specs=tuple(VMEM if shape.shape[0] < rows else HBM for shape in shapes),
        scratch_shapes=scratch,
        input_output_aliases=aliases,
        compiler_params=pltpu.CompilerParams(vmem_limit_bytes=16 << 20),
        cost_estimate=pl.CostEstimate(flops=flops, bytes_accessed=count * half * cols * 6, transcendentals=0),
        name=name,
    )(*inputs)


def local(features, weight, bias):
    rows, cols, owned, chans = features.shape
    count = lax.axis_size("tile")
    swap = [(0, 1), (1, 0)]
    own = jnp.transpose(features, (0, 2, 3, 1)).reshape(rows, owned * chans, cols)
    other = lax.ppermute(own, "rot", swap)
    near, far, weight = pick_edges(own, weight)

    def pairs(start):
        return [p for k in range(start, count - 1, 2) for p in ((k, k + 1), (k + 1, k))]

    near_own = lax.ppermute(near, "tile", pairs(0))
    far_own = lax.ppermute(far, "tile", pairs(1))
    filt, column = build_filters(weight, bias.reshape(1, chans), owned)
    split = rows // 2 + 1
    line = (owned * weight.shape[3], cols)

    def block(n):
        return jax.ShapeDtypeStruct((n,) + line, jnp.bfloat16)

    inputs = (filt, column, own, other)
    dma = pltpu.SemaphoreType.DMA
    (done,) = call(first_kernel, "first", (block(split - 1),), inputs, [], {}, split - 1)
    near_own, far_own, done = lax.optimization_barrier((near_own, far_own, done))
    halo = jnp.concatenate([near_own, far_own], 0)
    halo_other = lax.ppermute(halo, "rot", swap)
    more = rows - 1 - split
    out, done = call(second_kernel, "second", (block(rows), block(more)), inputs + (done,), [dma], {}, more)
    (out,) = call(
        last_kernel,
        "last",
        (block(rows),),
        inputs + (halo, halo_other, done, out),
        [pltpu.VMEM((2,) + line, jnp.bfloat16), dma, dma((2,))],
        {7: 0},
        2,
    )
    return jnp.transpose(out.reshape(rows, owned, chans, cols), (0, 3, 1, 2))


def solution(mesh):
    spec = P(("groups", "tile"), None, "rot", None)
    return jax.shard_map(
        local,
        mesh=mesh,
        in_specs=(spec, P(), P()),
        out_specs=spec,
        check_vma=False,
    )
```
